32 devices in a mesh: batch: 2 (over x), seq: 16 (over z, y, core).
Axes of the slice: x: 2, y: 2, z: 4, core: 2. Of those that a mesh axis runs over, the one named last changes fastest.
Arguments:
- inputs: bfloat16 [2, 2048, 1024], P('batch', 'seq'), may hold values from -6 to 6
- seg_ids: int32 [2, 2048], P('batch', 'seq'), may hold values from 0 to 3, never falling along the last dimension, each value on 1 to 1024 neighbouring positions
- gain_attn: bfloat16 [1024], P('batch'), may hold values from 0.5 to 1.5
- w_query: bfloat16 [1024, 512], P('batch'), may hold values from -0.1875 to 0.1875
- w_key: bfloat16 [1024, 512], P('batch'), may hold values from -0.1875 to 0.1875
- w_value: bfloat16 [1024, 1024], P('batch'), may hold values from -0.1875 to 0.1875
- w_outgate: bfloat16 [1024, 1024], P('batch'), may hold values from -0.1875 to 0.1875
- w_rank_in: bfloat16 [1024, 16], P('batch'), may hold values from -0.1875 to 0.1875
- w_rank_out: bfloat16 [16, 512], P(None, 'batch'), may hold values from -1.5 to 1.5
- rank_bias: bfloat16 [512], P('batch'), may hold values from -0.5 to 6
- head_gain: bfloat16 [256], P('batch'), may hold values from 0.5 to 1.5
- w_output: bfloat16 [1024, 1024], P(None, 'batch'), may hold values from -0.1875 to 0.1875
- gain_ffn: bfloat16 [1024], P('batch'), may hold values from 0.5 to 1.5
- w_gate: bfloat16 [1024, 2816], P('batch'), may hold values from -0.1875 to 0.1875
- w_up: bfloat16 [1024, 2816], P('batch'), may hold values from -0.1875 to 0.1875
- w_down: bfloat16 [2816, 1024], P('batch'), may hold values from -0.109375 to 0.109375
- cotangent: bfloat16 [2, 2048, 1024], P('batch', 'seq'), may hold values from -6 to 6
Outputs:
- output: bfloat16 [2, 2048, 1024], P('batch', 'seq')
- grad_inputs: bfloat16 [2, 2048, 1024], P('batch', 'seq')
- grad_gain_attn: float32 [1024], P('batch')
- grad_w_query: float32 [1024, 512], P('batch')
- grad_w_key: float32 [1024, 512], P('batch')
- grad_w_value: float32 [1024, 1024], P('batch')
- grad_w_outgate: float32 [1024, 1024], P('batch')
- grad_w_rank_in: float32 [1024, 16], P('batch')
- grad_w_rank_out: float32 [16, 512], P(None, 'batch')
- grad_rank_bias: float32 [512], P('batch')
- grad_head_gain: float32 [256], P('batch')
- grad_w_output: float32 [1024, 1024], P(None, 'batch')
- grad_gain_ffn: float32 [1024], P('batch')
- grad_w_gate: float32 [1024, 2816], P('batch')
- grad_w_up: float32 [1024, 2816], P('batch')
- grad_w_down: float32 [2816, 1024], P('batch')
The draws below stay inside these ranges and needn't reach their ends.
Inputs may be any that keep to these rules, and one draw needn't show every extreme that they name: `seg_ids`: along each sequence document ids never fall; each document holds 1 to 1024 tokens and one holds exactly 1024.
All inputs are finite; a program needn't handle non-finite values.
Results may differ from the reference program's by a relative error of at most 0.023.
Values may be sent and summed in bfloat16 or wider, within the bound.
A program may use at most 192 MiB of HBM per device.

```python
import math
import jax
import jax.numpy as jnp
import numpy as np
from jax import lax

D = 1024
HEADS = 4
DK = 128
DV = 256
RANK = 16
FF = 2816
SPAN = 64
KEYS = 512
VALS = 1024
SEQ_LEN = 2048
SEQS = 2
SEG_MOST = 1024
SEG_COUNT = 4


def draw_rank_bias(key, part):
    pick_key, fast_key, slow_key = jax.random.split(key, 3)
    share = 0.5
    slow_pick = jax.random.bernoulli(pick_key, share, (KEYS,))
    fast_vals = jax.random.uniform(fast_key, (KEYS,), jnp.float32, -0.5, 1.0)
    slow_base = min(math.log(SEG_MOST / 37.0), 3.5) + 1.5
    slow_vals = slow_base + jax.random.uniform(slow_key, (KEYS,), jnp.float32)
    return jnp.where(slow_pick, slow_vals, fast_vals).astype(jnp.bfloat16)


def level_of(own_key, extent, cuts, least, top_value):
    def one(dim, parts):
        steps = jax.random.uniform(jax.random.fold_in(jax.random.fold_in(own_key, 6), dim), (parts,), jnp.float32, least / len(cuts), top_value / len(cuts))
        return jnp.repeat(jnp.exp(steps), extent[dim] // parts).reshape((-1,) + (1,) * (len(extent) - dim - 1))

    level = one(*cuts[0])
    for cut in cuts[1:]:
        level = level * one(*cut)
    return level


def length_profile(amount, total, bound, slope):
    loads = [(1 << 20) // math.isqrt(standing ** slope) + 1 for standing in range(2, amount + 1)]
    spare, counts = total - bound - (amount - 1), [1] * (amount - 1)
    while spare > 0:
        candidates = [i for i in range(amount - 1) if counts[i] < bound]
        mass, left = sum([loads[i] for i in candidates]), spare
        for i in candidates:
            extra = min(bound - counts[i], max(1, left * loads[i] // mass), spare)
            counts[i] = counts[i] + extra
            spare = spare - extra
    return np.array([bound] + counts)


def ragged(stream_key, amount, total, most, skew):
    if amount == 2:
        one = jax.random.randint(stream_key, (), max(1, total - most), min(most, total - 1) + 1)
        return jnp.stack([one, total - one])
    lengths = jnp.asarray(length_profile(amount, total, most, skew), jnp.int32)
    twos = (amount - 1) // 2
    donor, sink = lengths[1:1 + 2 * twos:2], lengths[2:2 + 2 * twos:2]
    slack = jnp.minimum(donor - 1, most - sink)
    moved = jax.random.randint(jax.random.fold_in(stream_key, 1), (twos,), 0, 1 << 20) % (slack + 1)
    lengths = lengths.at[1:1 + 2 * twos:2].set(donor - moved).at[2:2 + 2 * twos:2].set(sink + moved)
    return lengths[jax.random.permutation(jax.random.fold_in(stream_key, 2), amount)]


def gaussian(own_key, dims, deviation, reach, shards=(), dtype=jnp.bfloat16):
    drawn = jax.random.normal(own_key, dims, jnp.float32) * deviation
    if len(shards) > 0:
        drawn = level_of(own_key, dims, shards, -0.22, 0.18) * drawn
    return jnp.clip(drawn, min=-reach, max=reach).astype(dtype)


def setup_inputs(seed: int = 0) -> dict:
    arg_keys = jax.random.split(jax.random.key(seed), 18)
    inputs = gaussian(arg_keys[0], (SEQS, SEQ_LEN, D), 1.0, 6.0, ((0, 2), (1, 16)))
    seg_ids = jax.vmap(lambda own: jnp.searchsorted(jnp.cumsum(ragged(own, SEG_COUNT, SEQ_LEN, SEG_MOST, 2)), jnp.arange(SEQ_LEN), side="right"))(jax.random.split(arg_keys[1], SEQS)).reshape((SEQS, SEQ_LEN)).astype(jnp.int32)
    gain_attn = jnp.clip(1.0 + 0.1 * jax.random.normal(arg_keys[2], (D,), jnp.float32), 0.5, 1.5).astype(jnp.bfloat16)
    w_query = gaussian(arg_keys[3], (D, KEYS), D ** -0.5, 0.1875, ((0, 2),))
    w_key = gaussian(arg_keys[4], (D, KEYS), D ** -0.5, 0.1875, ((0, 2),))
    w_value = gaussian(arg_keys[5], (D, VALS), D ** -0.5, 0.1875, ((0, 2),))
    w_outgate = gaussian(arg_keys[6], (D, VALS), D ** -0.5, 0.1875, ((0, 2),))
    w_rank_in = gaussian(arg_keys[7], (D, RANK), D ** -0.5, 0.1875, ((0, 2),))
    w_rank_out = gaussian(arg_keys[8], (RANK, KEYS), RANK ** -0.5, 1.5, ((1, 2),))
    rank_bias = draw_rank_bias(jax.random.fold_in(arg_keys[17], 71), 0)
    head_gain = jnp.clip(1.0 + 0.1 * jax.random.normal(arg_keys[10], (DV,), jnp.float32), 0.5, 1.5).astype(jnp.bfloat16)
    w_output = gaussian(arg_keys[11], (VALS, D), VALS ** -0.5, 0.1875, ((1, 2),))
    gain_ffn = jnp.clip(1.0 + 0.1 * jax.random.normal(arg_keys[12], (D,), jnp.float32), 0.5, 1.5).astype(jnp.bfloat16)
    w_gate = gaussian(arg_keys[13], (D, FF), D ** -0.5, 0.1875, ((0, 2),))
    w_up = gaussian(arg_keys[14], (D, FF), D ** -0.5, 0.1875, ((0, 2),))
    w_down = gaussian(arg_keys[15], (FF, D), FF ** -0.5, 0.109375, ((0, 2),))
    cotangent = gaussian(arg_keys[16], (SEQS, SEQ_LEN, D), 1.0, 6.0, ((0, 2), (1, 16)))
    return {"inputs": inputs, "seg_ids": seg_ids, "gain_attn": gain_attn, "w_query": w_query, "w_key": w_key, "w_value": w_value, "w_outgate": w_outgate, "w_rank_in": w_rank_in, "w_rank_out": w_rank_out, "rank_bias": rank_bias, "head_gain": head_gain, "w_output": w_output, "gain_ffn": gain_ffn, "w_gate": w_gate, "w_up": w_up, "w_down": w_down, "cotangent": cotangent}


norm_eps = 1e-05
head_eps = 0.1
top_prec = lax.Precision.HIGHEST

def rms_scale(values_in):
    return lax.rsqrt(lax.optimization_barrier(jnp.mean(values_in * values_in, axis=-1, keepdims=True)) + norm_eps)

def head_rms(values_in):
    return lax.rsqrt(lax.optimization_barrier(jnp.mean(values_in * values_in, axis=-1, keepdims=True)) + head_eps)

def span_step(carried_in, inputs_now):
    state_now, prior_id = carried_in
    queries, key_rows, value_rows, decays, seg_now = inputs_now
    span_len = queries.shape[0]
    cumulative = jnp.cumsum(decays, axis=0)
    first_id = seg_now[0]
    state_now = state_now * (prior_id == first_id).astype(jnp.float32)
    within_doc = (seg_now == first_id).astype(jnp.float32)
    query_dec = queries * jnp.exp(cumulative)
    key_dec = key_rows * jnp.exp(-cumulative)
    scores = jnp.einsum('thc,shc->hts', query_dec, key_dec, precision=top_prec)
    row_pos = lax.broadcasted_iota(jnp.int32, (span_len, span_len), 0)
    col_pos = lax.broadcasted_iota(jnp.int32, (span_len, span_len), 1)
    allowed = jnp.logical_and(col_pos <= row_pos, seg_now[:, None] == seg_now[None, :]).astype(jnp.float32)
    scores = scores * allowed[None]
    span_out = jnp.einsum('hts,shv->thv', scores, value_rows, precision=top_prec)
    span_out = span_out + within_doc[:, None, None] * jnp.einsum('thc,hcv->thv', query_dec, state_now, precision=top_prec)
    last_cumul = cumulative[-1]
    end_doc = (seg_now == seg_now[-1]).astype(jnp.float32)
    key_end = key_rows * jnp.exp(last_cumul[None] - cumulative) * end_doc[:, None, None]
    next_state = (jnp.exp(last_cumul) * within_doc[-1])[:, :, None] * state_now
    next_state = next_state + jnp.einsum('shc,shv->hcv', key_end, value_rows, precision=top_prec)
    return ((next_state, seg_now[-1]), span_out)

def gla_run(queries, key_rows, value_rows, decays, seg_row, start_state, prior_id):
    tok_count = queries.shape[0]
    num_spans = tok_count // SPAN

    def blocks(array_in):
        return array_in.reshape((num_spans, SPAN) + array_in.shape[1:])
    (final_state, last_id), outs_all = lax.scan(span_step, (start_state, prior_id), (blocks(queries), blocks(key_rows), blocks(value_rows), blocks(decays), seg_row.reshape(num_spans, SPAN)))
    return (outs_all.reshape((tok_count,) + outs_all.shape[2:]), final_state)

def silu_grad(pre_act, sig_val):
    return sig_val * (1.0 + pre_act * (1.0 - sig_val))

def sequence_pass(activ_in, seg_row, cot_rows, params):
    gain_one, query_w, key_w, value_w, outgate_w, rank_in_w, rank_out_w, bias_w, headgain_w, output_w, gain_two, gate_w, up_w, down_w = params
    f32 = jnp.float32
    bf16 = jnp.bfloat16
    activation = activ_in.astype(f32)
    tok_count = activation.shape[0]
    scale_one = rms_scale(activation)
    unit_one = activation * scale_one
    normed = (unit_one * gain_one.astype(f32)).astype(bf16)
    queries = jnp.dot(normed, query_w, preferred_element_type=f32) * DK ** (-0.5)
    keys_all = jnp.dot(normed, key_w, preferred_element_type=f32)
    values_all = jnp.dot(normed, value_w, preferred_element_type=f32)
    outgate = jnp.dot(normed, outgate_w, preferred_element_type=f32)
    low_rank = jnp.dot(normed, rank_in_w, preferred_element_type=f32)
    logits = jnp.dot(low_rank, rank_out_w.astype(f32), precision=top_prec) + bias_w.astype(f32)
    decays = jax.nn.log_sigmoid(logits) / 16.0

    def attention_core(queries_h, keys_h, values_h, decays_h):
        outs_all, final_state = gla_run(queries_h, keys_h, values_h, decays_h, seg_row, jnp.zeros((HEADS, DK, DV), f32), jnp.int32(-1))
        return outs_all
    attn_raw, pullback = jax.vjp(attention_core, queries.reshape(tok_count, HEADS, DK), keys_all.reshape(tok_count, HEADS, DK), values_all.reshape(tok_count, HEADS, DV), decays.reshape(tok_count, HEADS, DK))
    head_scale = head_rms(attn_raw)
    head_norm = attn_raw * head_scale
    gate_h = outgate.reshape(tok_count, HEADS, DV)
    gate_sig = jax.nn.sigmoid(gate_h)
    gate_act = gate_h * gate_sig
    head_gain32 = headgain_w.astype(f32)
    gated = (head_norm * head_gain32 * gate_act).reshape(tok_count, VALS).astype(bf16)
    resid = activation + jnp.dot(gated, output_w, preferred_element_type=f32)
    scale_two = rms_scale(resid)
    unit_two = resid * scale_two
    normed_two = (unit_two * gain_two.astype(f32)).astype(bf16)
    gate_pre = jnp.dot(normed_two, gate_w, preferred_element_type=f32)
    up_pre = jnp.dot(normed_two, up_w, preferred_element_type=f32)
    ffn_sig = jax.nn.sigmoid(gate_pre)
    hidden = (gate_pre * ffn_sig * up_pre).astype(bf16)
    output = (resid + jnp.dot(hidden, down_w, preferred_element_type=f32)).astype(bf16)
    grad_down = jnp.dot(hidden.T, cot_rows, preferred_element_type=f32)
    grad_hidden = jnp.dot(cot_rows, down_w.T, preferred_element_type=f32)
    grad_gate_pre = (grad_hidden * up_pre * silu_grad(gate_pre, ffn_sig)).astype(bf16)
    grad_up_pre = (grad_hidden * gate_pre * ffn_sig).astype(bf16)
    grad_gate = jnp.dot(normed_two.T, grad_gate_pre, preferred_element_type=f32)
    grad_up = jnp.dot(normed_two.T, grad_up_pre, preferred_element_type=f32)
    grad_normed_two = jnp.dot(grad_gate_pre, gate_w.T, preferred_element_type=f32) + jnp.dot(grad_up_pre, up_w.T, preferred_element_type=f32)
    grad_gain_two = lax.optimization_barrier(jnp.sum(grad_normed_two * unit_two, axis=0))
    scaled_two = grad_normed_two * gain_two.astype(f32)
    grad_resid = cot_rows.astype(f32) + scale_two * (scaled_two - unit_two * lax.optimization_barrier(jnp.mean(scaled_two * unit_two, axis=-1, keepdims=True)))
    resid_bf = grad_resid.astype(bf16)
    grad_output = jnp.dot(gated.T, resid_bf, preferred_element_type=f32)
    grad_gated = jnp.dot(resid_bf, output_w.T, preferred_element_type=f32).reshape(tok_count, HEADS, DV)
    grad_headgain = lax.optimization_barrier(jnp.sum(grad_gated * head_norm * gate_act, axis=(0, 1)))
    grad_gate_h = grad_gated * head_norm * head_gain32 * silu_grad(gate_h, gate_sig)
    grad_norm_h = grad_gated * head_gain32 * gate_act
    grad_attn = head_scale * (grad_norm_h - head_norm * lax.optimization_barrier(jnp.mean(grad_norm_h * head_norm, axis=-1, keepdims=True)))
    grad_q, grad_k, grad_v, grad_d = pullback(grad_attn)
    grad_logits = grad_d.reshape(tok_count, KEYS) * jax.nn.sigmoid(-logits) / 16.0
    grad_bias = lax.optimization_barrier(jnp.sum(grad_logits, axis=0))
    grad_rank_out = jnp.dot(low_rank.T, grad_logits, precision=top_prec)
    grad_low = jnp.dot(grad_logits, rank_out_w.astype(f32).T, precision=top_prec).astype(bf16)
    query_grad = (grad_q.reshape(tok_count, KEYS) * DK ** (-0.5)).astype(bf16)
    key_grad = grad_k.reshape(tok_count, KEYS).astype(bf16)
    value_grad = grad_v.reshape(tok_count, VALS).astype(bf16)
    outgate_grad = grad_gate_h.reshape(tok_count, VALS).astype(bf16)
    grad_query = jnp.dot(normed.T, query_grad, preferred_element_type=f32)
    grad_key = jnp.dot(normed.T, key_grad, preferred_element_type=f32)
    grad_value = jnp.dot(normed.T, value_grad, preferred_element_type=f32)
    grad_outgate = jnp.dot(normed.T, outgate_grad, preferred_element_type=f32)
    grad_rank_in = jnp.dot(normed.T, grad_low, preferred_element_type=f32)
    grad_normed = jnp.dot(query_grad, query_w.T, preferred_element_type=f32) + jnp.dot(key_grad, key_w.T, preferred_element_type=f32) + jnp.dot(value_grad, value_w.T, preferred_element_type=f32) + jnp.dot(outgate_grad, outgate_w.T, preferred_element_type=f32) + jnp.dot(grad_low, rank_in_w.T, preferred_element_type=f32)
    grad_gain_one = lax.optimization_barrier(jnp.sum(grad_normed * unit_one, axis=0))
    scaled_one = grad_normed * gain_one.astype(f32)
    grad_input = (grad_resid + scale_one * (scaled_one - unit_one * lax.optimization_barrier(jnp.mean(scaled_one * unit_one, axis=-1, keepdims=True)))).astype(bf16)
    grads = (grad_gain_one, grad_query, grad_key, grad_value, grad_outgate, grad_rank_in, grad_rank_out, grad_bias, grad_headgain, grad_output, grad_gain_two, grad_gate, grad_up, grad_down)
    return (output, grad_input, grads)

def reference(inputs, seg_ids, gain_attn, w_query, w_key, w_value, w_outgate, w_rank_in, w_rank_out, rank_bias, head_gain, w_output, gain_ffn, w_gate, w_up, w_down, cotangent):
    params = (gain_attn, w_query, w_key, w_value, w_outgate, w_rank_in, w_rank_out, rank_bias, head_gain, w_output, gain_ffn, w_gate, w_up, w_down)
    empty_grads = tuple((jnp.zeros(param.shape, jnp.float32) for param in params))

    def per_sequence(totals, items):
        out_rows, grad_rows, grads = sequence_pass(items[0], items[1], items[2], params)
        return (tuple((left + right for left, right in zip(totals, grads))), (out_rows, grad_rows))
    totals, outs_pair = lax.scan(per_sequence, empty_grads, (inputs, seg_ids, cotangent))
    return (outs_pair[0], outs_pair[1], totals[0], totals[1], totals[2], totals[3], totals[4], totals[5], totals[6], totals[7], totals[8], totals[9], totals[10], totals[11], totals[12], totals[13])
```

```python
import jax
import jax.numpy as jnp
from jax import lax
from jax.sharding import PartitionSpec as P

HEADS = 4
DK = 128
DV = 256
SPAN = 64
KEYS = 512
VALS = 1024


norm_eps = 1e-05
head_eps = 0.1
top_prec = lax.Precision.HIGHEST
BOTH = ("batch", "seq")


def rms_scale(values_in):
    return lax.rsqrt(jnp.mean(values_in * values_in, axis=-1, keepdims=True) + norm_eps)


def head_rms(values_in):
    return lax.rsqrt(jnp.mean(values_in * values_in, axis=-1, keepdims=True) + head_eps)


def silu_grad(pre_act, sig_val):
    return sig_val * (1.0 + pre_act * (1.0 - sig_val))


def mm(eq, a, b):
    return jnp.einsum(eq, a, b, precision=top_prec)


def own_piece(shard):
    rows = shard.shape[0] // lax.axis_size("seq")
    return lax.dynamic_slice_in_dim(shard, lax.axis_index("seq") * rows, rows, 0)


def gather_rows(shards):
    pieces = [own_piece(shard) for shard in shards]
    piece = pieces[0] if len(pieces) == 1 else jnp.concatenate(pieces, axis=1)
    return lax.all_gather(piece, BOTH, axis=0, tiled=True)


def sum_rows(partial):
    piece = lax.psum_scatter(
        partial.astype(jnp.bfloat16), BOTH, scatter_dimension=0, tiled=True
    )
    return lax.all_gather(piece, "seq", axis=0, tiled=True)


def to_spans(array_in, width):
    return array_in.reshape(-1, SPAN, HEADS, width).transpose(0, 2, 1, 3)


def from_spans(array_in):
    spans, heads, span_len, width = array_in.shape
    return array_in.transpose(0, 2, 1, 3).reshape(spans * span_len, heads * width)


def per_device(
    inputs,
    seg_ids,
    gain_attn,
    w_query,
    w_key,
    w_value,
    w_outgate,
    w_rank_in,
    w_rank_out,
    rank_bias,
    head_gain,
    w_output,
    gain_ffn,
    w_gate,
    w_up,
    w_down,
    cotangent,
):
    f32 = jnp.float32
    bf16 = jnp.bfloat16
    nb = lax.axis_size("batch")
    mine_b = lax.axis_index("batch")
    place = lax.axis_index("seq")
    peers = lax.axis_size("seq")

    small = (gain_attn, gain_ffn, rank_bias, head_gain, w_rank_in, w_rank_out)
    packed = jnp.concatenate([a.reshape(-1) for a in small])
    packed = lax.all_gather(packed, "batch", axis=0)
    parts, at = [], 0
    for a in small:
        parts.append(packed[:, at : at + a.size])
        at += a.size
    gain_one = parts[0].reshape(-1).astype(f32)
    gain_two = parts[1].reshape(-1).astype(f32)
    bias_w = parts[2].reshape(-1).astype(f32)
    head_gain32 = parts[3].reshape(-1).astype(f32)
    rank_in_w = parts[4].reshape(-1, w_rank_in.shape[1])
    rank_out_w = (
        parts[5].reshape((nb,) + w_rank_out.shape).transpose(1, 0, 2)
        .reshape(w_rank_out.shape[0], -1)
        .astype(f32)
    )
    proj_w = gather_rows((w_query, w_key, w_value, w_outgate))
    output_w = gather_rows((w_output,)).reshape((nb,) + w_output.shape)
    gate_up_w = gather_rows((w_gate, w_up))
    down_w = gather_rows((w_down,))
    ff = w_gate.shape[1]

    activation = inputs[0].astype(f32)
    seg_row = seg_ids[0]
    tok_count = activation.shape[0]
    spans = tok_count // SPAN
    scale_one = rms_scale(activation)
    unit_one = activation * scale_one
    normed = (unit_one * gain_one).astype(bf16)

    low_rank = jnp.dot(normed, rank_in_w, preferred_element_type=f32)
    logits = jnp.dot(low_rank, rank_out_w, precision=top_prec) + bias_w
    decays = jax.nn.log_sigmoid(logits) / 16.0

    seg_s = seg_row.reshape(spans, SPAN)
    first_s, last_s = seg_s[:, 0], seg_s[:, -1]
    row_pos = lax.broadcasted_iota(jnp.int32, (SPAN, SPAN), 0)
    col_pos = lax.broadcasted_iota(jnp.int32, (SPAN, SPAN), 1)
    lower = (col_pos <= row_pos).astype(f32)
    allowed = lower[None] * (seg_s[:, :, None] == seg_s[:, None, :]).astype(f32)
    allowed = allowed[:, None]
    prior = jnp.concatenate([seg_row[:1], last_s[:-1]])
    enters = (first_s == prior).astype(f32)
    within = ((seg_s == first_s[:, None]).astype(f32) * enters[:, None])[:, None, :, None]
    end_doc = (seg_s == last_s[:, None]).astype(f32)[:, None, :, None]

    cumul = mm("ts,nsc->ntc", lower, decays.reshape(spans, SPAN, KEYS))
    total_log = jnp.sum(cumul[:, -1], axis=0)
    edges = jnp.stack([seg_row[0], seg_row[-1]]).astype(f32)
    notes = lax.all_gather(jnp.concatenate([total_log, edges]), "seq", axis=0)
    all_log, firsts, lasts = notes[:, :KEYS], notes[:, KEYS], notes[:, KEYS + 1]

    proj = jnp.dot(normed, proj_w, preferred_element_type=f32)
    queries = to_spans(proj[:, :KEYS] * DK ** (-0.5), DK)
    keys_s = to_spans(proj[:, KEYS : 2 * KEYS], DK)
    values_s = to_spans(proj[:, 2 * KEYS : 2 * KEYS + VALS], DV)
    outgate = proj[:, 2 * KEYS + VALS :]

    cumul = cumul.reshape(spans, SPAN, HEADS, DK).transpose(0, 2, 1, 3)
    last_cumul = cumul[:, :, -1:, :]
    grow = jnp.exp(cumul)
    shrink = jnp.exp(-cumul)
    to_end = jnp.exp(last_cumul - cumul) * end_doc
    query_dec = queries * grow
    key_dec = keys_s * shrink
    key_end = keys_s * to_end
    query_in = query_dec * within
    keep = jnp.exp(last_cumul[:, :, 0, :]) * within[:, :, -1]
    scores = mm("nhtc,nhsc->nhts", query_dec, key_dec) * allowed
    local_out = mm("nhts,nhsv->nhtv", scores, values_s)
    added = mm("nhsc,nhsv->nhcv", key_end, values_s)

    local_state = added[0]
    for i in range(1, spans):
        local_state = keep[i][:, :, None] * local_state + added[i]
    states = lax.all_gather(local_state.astype(bf16), "seq", axis=0)

    before = lax.broadcasted_iota(jnp.int32, (peers, peers), 1)
    row = lax.broadcasted_iota(jnp.int32, (peers, peers), 0)
    order = jnp.arange(peers)
    between = jnp.logical_and(before > row, before < place).astype(f32)
    reach = jnp.logical_and(order < place, lasts == edges[0]).astype(f32)
    weight = jnp.exp(mm("ji,ic->jc", between, all_log)) * reach[:, None]
    carried = jnp.sum(
        states.astype(f32) * weight.reshape(peers, HEADS, DK, 1), axis=0
    )
    enter_list = [carried]
    for i in range(spans - 1):
        enter_list.append(keep[i][:, :, None] * enter_list[i] + added[i])
    entered = jnp.stack(enter_list)

    attn_raw = from_spans(local_out + mm("nhtc,nhcv->nhtv", query_in, entered)).reshape(
        tok_count, HEADS, DV
    )
    head_scale = head_rms(attn_raw)
    head_norm = attn_raw * head_scale
    gate_h = outgate.reshape(tok_count, HEADS, DV)
    gate_sig = jax.nn.sigmoid(gate_h)
    gate_act = gate_h * gate_sig
    gated = (head_norm * head_gain32 * gate_act).reshape(tok_count, VALS).astype(bf16)
    out_proj = jnp.concatenate(
        [jnp.dot(gated, output_w[b], preferred_element_type=f32) for b in range(nb)], axis=1
    )
    resid = activation + out_proj
    scale_two = rms_scale(resid)
    unit_two = resid * scale_two
    normed_two = (unit_two * gain_two).astype(bf16)
    gate_up = jnp.dot(normed_two, gate_up_w, preferred_element_type=f32)
    gate_pre, up_pre = gate_up[:, :ff], gate_up[:, ff:]
    ffn_sig = jax.nn.sigmoid(gate_pre)
    hidden = (gate_pre * ffn_sig * up_pre).astype(bf16)
    output = (resid + jnp.dot(hidden, down_w, preferred_element_type=f32)).astype(bf16)

    cot_rows = cotangent[0]
    grad_down = sum_rows(jnp.dot(hidden.T, cot_rows, preferred_element_type=f32))
    grad_hidden = jnp.dot(cot_rows, down_w.T, preferred_element_type=f32)
    grad_gate_up = jnp.concatenate(
        [
            (grad_hidden * up_pre * silu_grad(gate_pre, ffn_sig)).astype(bf16),
            (grad_hidden * gate_pre * ffn_sig).astype(bf16),
        ],
        axis=1,
    )
    grad_gu = sum_rows(jnp.dot(normed_two.T, grad_gate_up, preferred_element_type=f32))
    grad_normed_two = jnp.dot(grad_gate_up, gate_up_w.T, preferred_element_type=f32)
    grad_gain_two = jnp.sum(grad_normed_two * unit_two, axis=0)
    scaled_two = grad_normed_two * gain_two
    grad_resid = cot_rows.astype(f32) + scale_two * (
        scaled_two - unit_two * jnp.mean(scaled_two * unit_two, axis=-1, keepdims=True)
    )
    resid_bf = grad_resid.astype(bf16)
    half = resid_bf.shape[1] // nb
    halves = [resid_bf[:, b * half : (b + 1) * half] for b in range(nb)]
    grad_output = sum_rows(
        jnp.concatenate(
            [jnp.dot(gated.T, part, preferred_element_type=f32) for part in halves], axis=0
        )
    )
    grad_gated = sum(
        jnp.dot(part, output_w[b].T, preferred_element_type=f32)
        for b, part in enumerate(halves)
    ).reshape(tok_count, HEADS, DV)
    grad_headgain = jnp.sum(grad_gated * head_norm * gate_act, axis=(0, 1))
    grad_gate_h = grad_gated * head_norm * head_gain32 * silu_grad(gate_h, gate_sig)
    grad_norm_h = grad_gated * head_gain32 * gate_act
    grad_attn = head_scale * (
        grad_norm_h - head_norm * jnp.mean(grad_norm_h * head_norm, axis=-1, keepdims=True)
    )
    grad_o = to_spans(grad_attn.reshape(tok_count, VALS), DV)

    reach_grad = mm("nhtc,nhtv->nhcv", query_in, grad_o)
    local_grad = reach_grad[spans - 1]
    for i in range(spans - 2, -1, -1):
        local_grad = keep[i][:, :, None] * local_grad + reach_grad[i]
    grads_in = lax.all_gather(local_grad.astype(bf16), "seq", axis=0)

    grad_scores = mm("nhtv,nhsv->nhts", grad_o, values_s) * allowed
    grad_qd = mm("nhts,nhsc->nhtc", grad_scores, key_dec)
    grad_qd = grad_qd + within * mm("nhtv,nhcv->nhtc", grad_o, entered)
    grad_kd = mm("nhts,nhtc->nhsc", grad_scores, query_dec)
    grad_v = mm("nhts,nhtv->nhsv", scores, grad_o)

    between = jnp.logical_and(before < row, before > place).astype(f32)
    reach = jnp.logical_and(order > place, firsts == edges[1]).astype(f32)
    weight = jnp.exp(mm("ji,ic->jc", between, all_log)) * reach[:, None]
    grad_end = jnp.sum(
        grads_in.astype(f32) * weight.reshape(peers, HEADS, DK, 1), axis=0
    )
    end_list = [grad_end]
    for i in range(spans - 1, 0, -1):
        end_list.append(keep[i][:, :, None] * end_list[-1] + reach_grad[i])
    ends = jnp.stack(end_list[::-1])

    grad_v = grad_v + mm("nhsc,nhcv->nhsv", key_end, ends)
    grad_ke = mm("nhsv,nhcv->nhsc", values_s, ends)
    moved = grad_ke * key_end
    grad_last = jnp.sum(moved, axis=2) + keep * jnp.sum(ends * entered, axis=3)
    grad_cumul = grad_qd * query_dec - grad_kd * key_dec - moved
    grad_d = mm("ts,nhtc->nhsc", lower, grad_cumul) + grad_last[:, :, None, :]
    grad_q = grad_qd * grow
    grad_k = grad_kd * shrink + grad_ke * to_end

    grad_logits = from_spans(grad_d) * jax.nn.sigmoid(-logits) / 16.0
    grad_bias = jnp.sum(grad_logits, axis=0)
    grad_rank_out = jnp.dot(low_rank.T, grad_logits, precision=top_prec)
    grad_low = jnp.dot(grad_logits, rank_out_w.T, precision=top_prec).astype(bf16)
    proj_grad = jnp.concatenate(
        [
            from_spans(grad_q * DK ** (-0.5)).astype(bf16),
            from_spans(grad_k).astype(bf16),
            from_spans(grad_v).astype(bf16),
            grad_gate_h.reshape(tok_count, VALS).astype(bf16),
        ],
        axis=1,
    )
    grad_proj = sum_rows(jnp.dot(normed.T, proj_grad, preferred_element_type=f32))
    grad_normed = jnp.dot(proj_grad, proj_w.T, preferred_element_type=f32) + jnp.dot(
        grad_low, rank_in_w.T, preferred_element_type=f32
    )
    grad_gain_one = jnp.sum(grad_normed * unit_one, axis=0)
    scaled_one = grad_normed * gain_one
    grad_input = (
        grad_resid
        + scale_one
        * (scaled_one - unit_one * jnp.mean(scaled_one * unit_one, axis=-1, keepdims=True))
    ).astype(bf16)
    grad_rank_in = jnp.dot(normed.T, grad_low, preferred_element_type=f32)

    by_owner = jnp.concatenate(
        [
            grad_gain_one.reshape(nb, -1),
            grad_gain_two.reshape(nb, -1),
            grad_bias.reshape(nb, -1),
            grad_headgain.reshape(nb, -1),
            grad_rank_in.reshape(nb, -1),
            grad_rank_out.reshape(w_rank_out.shape[0], nb, -1).transpose(1, 0, 2).reshape(nb, -1),
        ],
        axis=1,
    )
    owned = lax.dynamic_index_in_dim(lax.psum(by_owner, BOTH), mine_b, 0, False)
    outs, at = [], 0
    for a in small:
        outs.append(owned[at : at + a.size].reshape(a.shape))
        at += a.size
    g_gain_one, g_gain_two, g_bias, g_headgain, g_rank_in, g_rank_out = outs
    grad_proj = grad_proj.astype(f32)
    grad_gu = grad_gu.astype(f32)
    return (
        output[None],
        grad_input[None],
        g_gain_one,
        grad_proj[:, :KEYS],
        grad_proj[:, KEYS : 2 * KEYS],
        grad_proj[:, 2 * KEYS : 2 * KEYS + VALS],
        grad_proj[:, 2 * KEYS + VALS :],
        g_rank_in,
        g_rank_out,
        g_bias,
        g_headgain,
        grad_output.astype(f32),
        g_gain_two,
        grad_gu[:, :ff],
        grad_gu[:, ff:],
        grad_down.astype(f32),
    )


def solution(mesh):
    in_specs = (
        P("batch", "seq", None),
        P("batch", "seq"),
        P("batch"),
        P("batch", None),
        P("batch", None),
        P("batch", None),
        P("batch", None),
        P("batch", None),
        P(None, "batch"),
        P("batch"),
        P("batch"),
        P(None, "batch"),
        P("batch"),
        P("batch", None),
        P("batch", None),
        P("batch", None),
        P("batch", "seq", None),
    )
    out_specs = (
        P("batch", "seq", None),
        P("batch", "seq", None),
        P("batch"),
        P("batch", None),
        P("batch", None),
        P("batch", None),
        P("batch", None),
        P("batch", None),
        P(None, "batch"),
        P("batch"),
        P("batch"),
        P(None, "batch"),
        P("batch"),
        P("batch", None),
        P("batch", None),
        P("batch", None),
    )
    return jax.shard_map(
        per_device, mesh=mesh, in_specs=in_specs, out_specs=out_specs, check_vma=False
    )
```

```python
import jax
import jax.numpy as jnp
from jax import lax
from jax.sharding import PartitionSpec as P

HEADS = 4
DK = 128
DV = 256
SPAN = 64
KEYS = 512
VALS = 1024


norm_eps = 1e-05
head_eps = 0.1
top_prec = lax.Precision.HIGHEST
BOTH = ("batch", "seq")


def rms_scale(values_in):
    return lax.rsqrt(jnp.mean(values_in * values_in, axis=-1, keepdims=True) + norm_eps)


def head_rms(values_in):
    return lax.rsqrt(jnp.mean(values_in * values_in, axis=-1, keepdims=True) + head_eps)


def silu_grad(pre_act, sig_val):
    return sig_val * (1.0 + pre_act * (1.0 - sig_val))


def mm(eq, a, b):
    return jnp.einsum(eq, a, b, precision=top_prec)


def gather_rows(shards):
    piece = shards[0] if len(shards) == 1 else jnp.concatenate(shards, axis=1)
    return lax.all_gather(piece, "batch", axis=0, tiled=True)


def all_tokens(rows):
    return lax.all_gather(rows, "batch", axis=0, tiled=True)


def own_columns(rows):
    width = rows.shape[1] // lax.axis_size("batch")
    return lax.dynamic_slice_in_dim(rows, lax.axis_index("batch") * width, width, 1)


def own_grad(left, right):
    part = jnp.dot(left.T, right, preferred_element_type=jnp.float32)
    return lax.psum(part.astype(jnp.bfloat16), "seq")


def to_spans(array_in, width):
    return array_in.reshape(-1, SPAN, HEADS, width).transpose(0, 2, 1, 3)


def from_spans(array_in):
    spans, heads, span_len, width = array_in.shape
    return array_in.transpose(0, 2, 1, 3).reshape(spans * span_len, heads * width)


def per_device(
    inputs,
    seg_ids,
    gain_attn,
    w_query,
    w_key,
    w_value,
    w_outgate,
    w_rank_in,
    w_rank_out,
    rank_bias,
    head_gain,
    w_output,
    gain_ffn,
    w_gate,
    w_up,
    w_down,
    cotangent,
):
    f32 = jnp.float32
    bf16 = jnp.bfloat16
    nb = lax.axis_size("batch")
    mine_b = lax.axis_index("batch")
    place = lax.axis_index("seq")
    peers = lax.axis_size("seq")

    small = (gain_attn, gain_ffn, rank_bias, head_gain, w_rank_in, w_rank_out)
    packed = jnp.concatenate([a.reshape(-1) for a in small])
    packed = lax.all_gather(packed, "batch", axis=0)
    parts, at = [], 0
    for a in small:
        parts.append(packed[:, at : at + a.size])
        at += a.size
    gain_one = parts[0].reshape(-1).astype(f32)
    gain_two = parts[1].reshape(-1).astype(f32)
    bias_w = parts[2].reshape(-1).astype(f32)
    head_gain32 = parts[3].reshape(-1).astype(f32)
    rank_in_w = parts[4].reshape(-1, w_rank_in.shape[1])
    rank_out_w = (
        parts[5].reshape((nb,) + w_rank_out.shape).transpose(1, 0, 2)
        .reshape(w_rank_out.shape[0], -1)
        .astype(f32)
    )
    proj_w = gather_rows((w_query, w_key, w_value, w_outgate))
    output_w = gather_rows((w_output,)).reshape((nb,) + w_output.shape)
    gate_up_w = gather_rows((w_gate, w_up))
    down_w = gather_rows((w_down,))
    ff = w_gate.shape[1]

    activation = inputs[0].astype(f32)
    seg_row = seg_ids[0]
    tok_count = activation.shape[0]
    spans = tok_count // SPAN
    scale_one = rms_scale(activation)
    unit_one = activation * scale_one
    normed = (unit_one * gain_one).astype(bf16)

    low_rank = jnp.dot(normed, rank_in_w, preferred_element_type=f32)
    logits = jnp.dot(low_rank, rank_out_w, precision=top_prec) + bias_w
    decays = jax.nn.log_sigmoid(logits) / 16.0

    seg_s = seg_row.reshape(spans, SPAN)
    first_s, last_s = seg_s[:, 0], seg_s[:, -1]
    row_pos = lax.broadcasted_iota(jnp.int32, (SPAN, SPAN), 0)
    col_pos = lax.broadcasted_iota(jnp.int32, (SPAN, SPAN), 1)
    lower = (col_pos <= row_pos).astype(f32)
    allowed = lower[None] * (seg_s[:, :, None] == seg_s[:, None, :]).astype(f32)
    allowed = allowed[:, None]
    prior = jnp.concatenate([seg_row[:1], last_s[:-1]])
    enters = (first_s == prior).astype(f32)
    within = ((seg_s == first_s[:, None]).astype(f32) * enters[:, None])[:, None, :, None]
    end_doc = (seg_s == last_s[:, None]).astype(f32)[:, None, :, None]

    cumul = mm("ts,nsc->ntc", lower, decays.reshape(spans, SPAN, KEYS))
    total_log = jnp.sum(cumul[:, -1], axis=0)
    edges = jnp.stack([seg_row[0], seg_row[-1]]).astype(f32)
    notes = lax.all_gather(jnp.concatenate([total_log, edges]), "seq", axis=0)
    all_log, firsts, lasts = notes[:, :KEYS], notes[:, KEYS], notes[:, KEYS + 1]

    proj = jnp.dot(normed, proj_w, preferred_element_type=f32)
    queries = to_spans(proj[:, :KEYS] * DK ** (-0.5), DK)
    keys_s = to_spans(proj[:, KEYS : 2 * KEYS], DK)
    values_s = to_spans(proj[:, 2 * KEYS : 2 * KEYS + VALS], DV)
    outgate = proj[:, 2 * KEYS + VALS :]

    cumul = cumul.reshape(spans, SPAN, HEADS, DK).transpose(0, 2, 1, 3)
    last_cumul = cumul[:, :, -1:, :]
    grow = jnp.exp(cumul)
    shrink = jnp.exp(-cumul)
    to_end = jnp.exp(last_cumul - cumul) * end_doc
    query_dec = queries * grow
    key_dec = keys_s * shrink
    key_end = keys_s * to_end
    query_in = query_dec * within
    keep = jnp.exp(last_cumul[:, :, 0, :]) * within[:, :, -1]
    scores = mm("nhtc,nhsc->nhts", query_dec, key_dec) * allowed
    local_out = mm("nhts,nhsv->nhtv", scores, values_s)
    added = mm("nhsc,nhsv->nhcv", key_end, values_s)

    local_state = added[0]
    for i in range(1, spans):
        local_state = keep[i][:, :, None] * local_state + added[i]
    states = lax.all_gather(local_state.astype(bf16), "seq", axis=0)

    before = lax.broadcasted_iota(jnp.int32, (peers, peers), 1)
    row = lax.broadcasted_iota(jnp.int32, (peers, peers), 0)
    order = jnp.arange(peers)
    between = jnp.logical_and(before > row, before < place).astype(f32)
    reach = jnp.logical_and(order < place, lasts == edges[0]).astype(f32)
    weight = jnp.exp(mm("ji,ic->jc", between, all_log)) * reach[:, None]
    carried = jnp.sum(
        states.astype(f32) * weight.reshape(peers, HEADS, DK, 1), axis=0
    )
    enter_list = [carried]
    for i in range(spans - 1):
        enter_list.append(keep[i][:, :, None] * enter_list[i] + added[i])
    entered = jnp.stack(enter_list)

    attn_raw = from_spans(local_out + mm("nhtc,nhcv->nhtv", query_in, entered)).reshape(
        tok_count, HEADS, DV
    )
    head_scale = head_rms(attn_raw)
    head_norm = attn_raw * head_scale
    gate_h = outgate.reshape(tok_count, HEADS, DV)
    gate_sig = jax.nn.sigmoid(gate_h)
    gate_act = gate_h * gate_sig
    gated = (head_norm * head_gain32 * gate_act).reshape(tok_count, VALS).astype(bf16)
    out_proj = jnp.concatenate(
        [jnp.dot(gated, output_w[b], preferred_element_type=f32) for b in range(nb)], axis=1
    )
    resid = activation + out_proj
    scale_two = rms_scale(resid)
    unit_two = resid * scale_two
    normed_two = (unit_two * gain_two).astype(bf16)
    gate_up = jnp.dot(normed_two, gate_up_w, preferred_element_type=f32)
    gate_pre, up_pre = gate_up[:, :ff], gate_up[:, ff:]
    ffn_sig = jax.nn.sigmoid(gate_pre)
    hidden = (gate_pre * ffn_sig * up_pre).astype(bf16)
    output = (resid + jnp.dot(hidden, down_w, preferred_element_type=f32)).astype(bf16)

    cot_rows = cotangent[0]
    grad_down = own_grad(own_columns(all_tokens(hidden)), all_tokens(cot_rows))
    grad_hidden = jnp.dot(cot_rows, down_w.T, preferred_element_type=f32)
    grad_gate_up = jnp.concatenate(
        [
            (grad_hidden * up_pre * silu_grad(gate_pre, ffn_sig)).astype(bf16),
            (grad_hidden * gate_pre * ffn_sig).astype(bf16),
        ],
        axis=1,
    )
    grad_gu = own_grad(own_columns(all_tokens(normed_two)), all_tokens(grad_gate_up))
    grad_normed_two = jnp.dot(grad_gate_up, gate_up_w.T, preferred_element_type=f32)
    grad_gain_two = jnp.sum(grad_normed_two * unit_two, axis=0)
    scaled_two = grad_normed_two * gain_two
    grad_resid = cot_rows.astype(f32) + scale_two * (
        scaled_two - unit_two * jnp.mean(scaled_two * unit_two, axis=-1, keepdims=True)
    )
    resid_bf = grad_resid.astype(bf16)
    half = resid_bf.shape[1] // nb
    halves = [resid_bf[:, b * half : (b + 1) * half] for b in range(nb)]
    grad_output = own_grad(all_tokens(gated), own_columns(all_tokens(resid_bf)))
    grad_gated = sum(
        jnp.dot(part, output_w[b].T, preferred_element_type=f32)
        for b, part in enumerate(halves)
    ).reshape(tok_count, HEADS, DV)
    grad_headgain = jnp.sum(grad_gated * head_norm * gate_act, axis=(0, 1))
    grad_gate_h = grad_gated * head_norm * head_gain32 * silu_grad(gate_h, gate_sig)
    grad_norm_h = grad_gated * head_gain32 * gate_act
    grad_attn = head_scale * (
        grad_norm_h - head_norm * jnp.mean(grad_norm_h * head_norm, axis=-1, keepdims=True)
    )
    grad_o = to_spans(grad_attn.reshape(tok_count, VALS), DV)

    reach_grad = mm("nhtc,nhtv->nhcv", query_in, grad_o)
    local_grad = reach_grad[spans - 1]
    for i in range(spans - 2, -1, -1):
        local_grad = keep[i][:, :, None] * local_grad + reach_grad[i]
    grads_in = lax.all_gather(local_grad.astype(bf16), "seq", axis=0)

    grad_scores = mm("nhtv,nhsv->nhts", grad_o, values_s) * allowed
    grad_qd = mm("nhts,nhsc->nhtc", grad_scores, key_dec)
    grad_qd = grad_qd + within * mm("nhtv,nhcv->nhtc", grad_o, entered)
    grad_kd = mm("nhts,nhtc->nhsc", grad_scores, query_dec)
    grad_v = mm("nhts,nhtv->nhsv", scores, grad_o)

    between = jnp.logical_and(before < row, before > place).astype(f32)
    reach = jnp.logical_and(order > place, firsts == edges[1]).astype(f32)
    weight = jnp.exp(mm("ji,ic->jc", between, all_log)) * reach[:, None]
    grad_end = jnp.sum(
        grads_in.astype(f32) * weight.reshape(peers, HEADS, DK, 1), axis=0
    )
    end_list = [grad_end]
    for i in range(spans - 1, 0, -1):
        end_list.append(keep[i][:, :, None] * end_list[-1] + reach_grad[i])
    ends = jnp.stack(end_list[::-1])

    grad_v = grad_v + mm("nhsc,nhcv->nhsv", key_end, ends)
    grad_ke = mm("nhsv,nhcv->nhsc", values_s, ends)
    moved = grad_ke * key_end
    grad_last = jnp.sum(moved, axis=2) + keep * jnp.sum(ends * entered, axis=3)
    grad_cumul = grad_qd * query_dec - grad_kd * key_dec - moved
    grad_d = mm("ts,nhtc->nhsc", lower, grad_cumul) + grad_last[:, :, None, :]
    grad_q = grad_qd * grow
    grad_k = grad_kd * shrink + grad_ke * to_end

    grad_logits = from_spans(grad_d) * jax.nn.sigmoid(-logits) / 16.0
    grad_bias = jnp.sum(grad_logits, axis=0)
    grad_rank_out = jnp.dot(low_rank.T, grad_logits, precision=top_prec)
    grad_low = jnp.dot(grad_logits, rank_out_w.T, precision=top_prec).astype(bf16)
    proj_grad = jnp.concatenate(
        [
            from_spans(grad_q * DK ** (-0.5)).astype(bf16),
            from_spans(grad_k).astype(bf16),
            from_spans(grad_v).astype(bf16),
            grad_gate_h.reshape(tok_count, VALS).astype(bf16),
        ],
        axis=1,
    )
    grad_proj = own_grad(own_columns(all_tokens(normed)), all_tokens(proj_grad))
    grad_normed = jnp.dot(proj_grad, proj_w.T, preferred_element_type=f32) + jnp.dot(
        grad_low, rank_in_w.T, preferred_element_type=f32
    )
    grad_gain_one = jnp.sum(grad_normed * unit_one, axis=0)
    scaled_one = grad_normed * gain_one
    grad_input = (
        grad_resid
        + scale_one
        * (scaled_one - unit_one * jnp.mean(scaled_one * unit_one, axis=-1, keepdims=True))
    ).astype(bf16)
    grad_rank_in = jnp.dot(normed.T, grad_low, preferred_element_type=f32)

    by_owner = jnp.concatenate(
        [
            grad_gain_one.reshape(nb, -1),
            grad_gain_two.reshape(nb, -1),
            grad_bias.reshape(nb, -1),
            grad_headgain.reshape(nb, -1),
            grad_rank_in.reshape(nb, -1),
            grad_rank_out.reshape(w_rank_out.shape[0], nb, -1).transpose(1, 0, 2).reshape(nb, -1),
        ],
        axis=1,
    )
    owned = lax.dynamic_index_in_dim(lax.psum(by_owner, BOTH), mine_b, 0, False)
    outs, at = [], 0
    for a in small:
        outs.append(owned[at : at + a.size].reshape(a.shape))
        at += a.size
    g_gain_one, g_gain_two, g_bias, g_headgain, g_rank_in, g_rank_out = outs
    grad_proj = grad_proj.astype(f32)
    grad_gu = grad_gu.astype(f32)
    return (
        output[None],
        grad_input[None],
        g_gain_one,
        grad_proj[:, :KEYS],
        grad_proj[:, KEYS : 2 * KEYS],
        grad_proj[:, 2 * KEYS : 2 * KEYS + VALS],
        grad_proj[:, 2 * KEYS + VALS :],
        g_rank_in,
        g_rank_out,
        g_bias,
        g_headgain,
        grad_output.astype(f32),
        g_gain_two,
        grad_gu[:, :ff],
        grad_gu[:, ff:],
        grad_down.astype(f32),
    )


def solution(mesh):
    in_specs = (
        P("batch", "seq", None),
        P("batch", "seq"),
        P("batch"),
        P("batch", None),
        P("batch", None),
        P("batch", None),
        P("batch", None),
        P("batch", None),
        P(None, "batch"),
        P("batch"),
        P("batch"),
        P(None, "batch"),
        P("batch"),
        P("batch", None),
        P("batch", None),
        P("batch", None),
        P("batch", "seq", None),
    )
    out_specs = (
        P("batch", "seq", None),
        P("batch", "seq", None),
        P("batch"),
        P("batch", None),
        P("batch", None),
        P("batch", None),
        P("batch", None),
        P("batch", None),
        P(None, "batch"),
        P("batch"),
        P("batch"),
        P(None, "batch"),
        P("batch"),
        P("batch", None),
        P("batch", None),
        P("batch", None),
    )
    return jax.shard_map(
        per_device, mesh=mesh, in_specs=in_specs, out_specs=out_specs, check_vma=False
    )
```
